256 devices in a mesh: seq: 32 (over z, y), head: 8 (over x, core).
Axes of the slice: x: 4, y: 4, z: 8, core: 2. Of those that a mesh axis runs over, the one named last changes fastest.
Arguments:
- x_in: bfloat16 [4096, 8192], P('seq', 'head'), may hold values from -6 to 6
- z_gate: bfloat16 [4096, 8192], P('seq', 'head'), may hold values from -6 to 6
- b_in: bfloat16 [4096, 2048], P('seq', 'head'), may hold values from -0.75 to 0.75
- c_in: bfloat16 [4096, 2048], P('seq', 'head'), may hold values from -0.75 to 0.75
- log_decay: float32 [4096, 128], P('seq', 'head'), may hold values from 0 to 1.5
- step_size: float32 [4096, 128], P('seq', 'head'), may hold values from 0.3 to 3
- d_skip: float32 [128], P('head'), may hold values from 0.5 to 2
- norm_gain: float32 [8192], P('head'), may hold values from 0.25 to 1.75
- w_out: bfloat16 [8192, 4096], P('head'), may hold values from -0.0625 to 0.0625
- residual: bfloat16 [4096, 4096], P(('seq', 'head')), may hold values from -8 to 8
- final_gain: float32 [4096], replicated, may hold values from 0.25 to 1.75
- vocab: bfloat16 [65536, 4096], P(('seq', 'head')), may hold values from -12 to 12
- targets: int32 [32, 128], P(None, 'head'), may hold values from 0 to 65535
Outputs:
- hidden_out: float32 [4096, 4096], P(('seq', 'head'))
- logprob: float32 [4096], P(('seq', 'head'))
The draws below stay inside these ranges and needn't reach their ends.
All inputs are finite; a program needn't handle non-finite values.
Results may differ from the reference program's by a relative error of at most 0.0029.
Values may be sent and summed in bfloat16 or wider, within the bound.
No kernel may reach another device: no remote copies, remote signals or barrier semaphores. Data moves between devices by JAX's collectives and lax.ppermute only.
A program may use at most 128 MiB of HBM per device.

```python
import math
import jax
import jax.numpy as jnp
from jax import lax

D = 4096
SCAN_LANE_NUMBER = 128
HEAD_DIM = 64
STATE = 256
GROUPS = 8
VOCAB = 65536
TOK_DEV = 128
INNER = 8192
CONTEXT_SPAN = 4096
SEQ_BLOCKS = 32


def shared_axis(key):
    vector = jax.random.normal(jax.random.fold_in(key, 4242), (D,), jnp.float32)
    return vector / jnp.sqrt(jnp.sum(vector * vector))


def draw_log_decay(key, part):
    keys = jax.random.split(key, 8)
    slow_edge = 0.55
    middle_edge = 0.85
    class_draw = jax.random.uniform(keys[0], (SCAN_LANE_NUMBER,))
    is_slow = class_draw < slow_edge
    is_middle = jnp.logical_and(class_draw >= slow_edge, class_draw < middle_edge)
    slow = jnp.exp(jax.random.uniform(keys[1], (SCAN_LANE_NUMBER,), jnp.float32, math.log(2e-05), math.log(0.0001)))
    middle = jnp.exp(jax.random.uniform(keys[7], (SCAN_LANE_NUMBER,), jnp.float32, math.log(0.0012), math.log(0.004)))
    quick = jnp.exp(jax.random.uniform(keys[2], (SCAN_LANE_NUMBER,), jnp.float32, math.log(0.02), math.log(0.033)))
    reference_speed = jnp.where(is_slow, slow, jnp.where(is_middle, middle, quick))
    block_count = CONTEXT_SPAN // TOK_DEV
    tile_factor = jnp.exp(jax.random.uniform(keys[3], (block_count, SCAN_LANE_NUMBER), jnp.float32, math.log(0.5), math.log(2.0)))
    tile_factor = jnp.repeat(tile_factor, TOK_DEV, axis=0)
    approximate_guess = jax.random.uniform(keys[4], (CONTEXT_SPAN, SCAN_LANE_NUMBER), jnp.float32, 0.5, 1.5)
    location_indices = jax.random.randint(keys[5], (3,), 0, CONTEXT_SPAN)
    quantity_list = jax.random.uniform(keys[6], (3, SCAN_LANE_NUMBER), jnp.float32, 0.22, 0.69)
    spike_lengths = jnp.zeros((CONTEXT_SPAN, SCAN_LANE_NUMBER), jnp.float32).at[location_indices].add(quantity_list)
    return reference_speed[None, :] * tile_factor * approximate_guess + spike_lengths


def draw_residual(key, part):
    keys = jax.random.split(jax.random.fold_in(key, 515), 2)
    coefficient = jax.random.uniform(keys[0], (CONTEXT_SPAN, 1), jnp.float32, -0.75, 0.75)
    noise = jnp.clip(jax.random.normal(keys[1], (CONTEXT_SPAN, D), jnp.float32), -6.0, 6.0)
    table = noise + coefficient * math.sqrt(D) * shared_axis(key)[None, :]
    return jnp.clip(table, -8.0, 8.0).astype(jnp.bfloat16)


def draw_vocab(key, part):
    keys = jax.random.split(key, 7)
    trend = 1.0 + 0.12 * jnp.arange(VOCAB, dtype=jnp.float32) / VOCAB
    approximate_guess = jnp.exp(jax.random.uniform(keys[0], (VOCAB, 1), jnp.float32, math.log(0.8), math.log(1.25)))
    table = jax.random.normal(keys[1], (VOCAB, D), jnp.float32) * (3.0 / math.sqrt(D)) * trend[:, None] * approximate_guess
    aligned_rows = jax.random.randint(keys[6], (8,), 0, VOCAB)
    magnitudes = jax.random.uniform(jax.random.fold_in(key, 77), (8,), jnp.float32, 0.35, 0.7)
    signs = jnp.where(jnp.arange(8) % 2 == 0, 1.0, -1.0)
    table = table.at[aligned_rows].set((signs * magnitudes)[:, None] * shared_axis(key)[None, :])
    table = jnp.clip(table, -12.0, 12.0)
    return table.astype(jnp.bfloat16)


def set_ends(drawn, key, low, high):
    longest = drawn.shape.index(max(drawn.shape))
    spots = []
    for shift in (0, 1):
        where = [jax.random.randint(jax.random.fold_in(key, axis), (), 0, length) for axis, length in enumerate(drawn.shape)]
        where[longest] = (where[longest] + shift) % drawn.shape[longest]
        spots.append(tuple(where))
    return drawn.at[spots[0]].set(low).at[spots[1]].set(high)


def steps_of(stream_key, shape, cuts, smallest, top_value):
    def one(axis_at, shards_of):
        steps = jax.random.uniform(jax.random.fold_in(jax.random.fold_in(stream_key, 6), axis_at), (shards_of,), jnp.float32, smallest / len(cuts), top_value / len(cuts))
        return jnp.repeat(jnp.exp(steps), shape[axis_at] // shards_of).reshape((-1,) + (1,) * (len(shape) - axis_at - 1))

    level = one(*cuts[0])
    for cut in cuts[1:]:
        level = level * one(*cut)
    return level


def bell_draw(rng, dims, scale, bound, shards=(), kind=jnp.bfloat16):
    values = jax.random.normal(rng, dims, jnp.float32) * scale
    if len(shards) > 0:
        values = steps_of(rng, dims, shards, -0.22, 0.18) * values
    return jnp.clip(values, min=-bound, max=bound).astype(kind)


def setup_inputs(seed: int = 0) -> dict:
    splits = jax.random.split(jax.random.key(seed), 14)
    x_in = bell_draw(splits[0], (CONTEXT_SPAN, INNER), 1.0, 6.0, ((0, 32), (1, 8)))
    z_gate = bell_draw(splits[1], (CONTEXT_SPAN, INNER), 1.0, 6.0, ((0, 32), (1, 8)))
    b_in = bell_draw(splits[2], (CONTEXT_SPAN, GROUPS * STATE), 0.125, 0.75, ((0, 32), (1, 8)))
    c_in = bell_draw(splits[3], (CONTEXT_SPAN, GROUPS * STATE), 0.125, 0.75, ((0, 32), (1, 8)))
    log_decay = draw_log_decay(jax.random.fold_in(splits[13], 71), 0)
    step_size = jnp.clip(jnp.exp(math.log(3.0) - 2.3025851 * jax.random.uniform(splits[5], (CONTEXT_SPAN, SCAN_LANE_NUMBER), jnp.float32) ** steps_of(splits[5], (CONTEXT_SPAN, SCAN_LANE_NUMBER), ((0, 32), (1, 8)), -0.2, 0.2)), 0.3, 3.0)
    d_skip = jnp.clip(0.5 + 1.5 * jax.random.uniform(splits[6], (SCAN_LANE_NUMBER,), jnp.float32) ** steps_of(splits[6], (SCAN_LANE_NUMBER,), ((0, 8),), -0.2, 0.2), 0.5, 2.0)
    norm_gain = jnp.clip(1.0 + 0.15 * jax.random.normal(splits[7], (INNER,), jnp.float32), 0.25, 1.75)
    w_out = bell_draw(splits[8], (INNER, D), INNER ** -0.5, 0.0625, ((0, 8),))
    residual = draw_residual(jax.random.fold_in(splits[13], 71), 0)
    final_gain = jnp.clip(1.0 + 0.15 * jax.random.normal(splits[10], (D,), jnp.float32), 0.25, 1.75)
    vocab = draw_vocab(jax.random.fold_in(splits[13], 71), 0)
    targets = set_ends(jax.random.randint(splits[12], (SEQ_BLOCKS, TOK_DEV), 0, VOCAB), jax.random.fold_in(splits[12], 1), 0, VOCAB - 1).astype(jnp.int32)
    return dict(x_in=x_in, z_gate=z_gate, b_in=b_in, c_in=c_in, log_decay=log_decay, step_size=step_size, d_skip=d_skip, norm_gain=norm_gain, w_out=w_out, residual=residual, final_gain=final_gain, vocab=vocab, targets=targets)


epsilon = 1e-05
highest = lax.Precision.HIGHEST

def local_terms(inputs, b_rows, c_rows, decays, step_rows, per_group):
    length = inputs.shape[0]
    cumulative = jnp.cumsum(decays, axis=0)
    by_head = cumulative.T
    gaps = by_head[:, None, :] - by_head[:, :, None]
    positions = jnp.arange(length)
    causal = positions[None, :] <= positions[:, None]
    segment_w = jnp.where(causal[None], jnp.exp(jnp.minimum(gaps, 0.0)), 0.0)
    scores = jnp.einsum('tgn,sgn->gts', c_rows, b_rows, precision=highest)
    head_scores = jnp.repeat(scores, per_group, axis=0)
    weights = segment_w * head_scores * step_rows.T[:, None, :]
    within = jnp.einsum('hts,shp->thp', weights, inputs, precision=highest)
    last = cumulative[-1]
    end_weight = jnp.exp(last[None, :] - cumulative) * step_rows
    b_heads = jnp.repeat(b_rows, per_group, axis=1)
    end_state = jnp.einsum('shp,shn->hpn', inputs * end_weight[:, :, None], b_heads, precision=highest)
    return (within, cumulative, end_state, jnp.exp(-last))

def carried(c_rows, cumulative, state, per_group):
    c_heads = jnp.repeat(c_rows, per_group, axis=1)
    return jnp.exp(-cumulative)[:, :, None] * jnp.einsum('thn,hpn->thp', c_heads, state, precision=highest)

def reference(x_in, z_gate, b_in, c_in, log_decay, step_size, d_skip, norm_gain, w_out, residual, final_gain, vocab, targets):
    per_group = SCAN_LANE_NUMBER // GROUPS
    blocks = CONTEXT_SPAN // TOK_DEV
    inputs = x_in.astype(jnp.float32).reshape(blocks, TOK_DEV, SCAN_LANE_NUMBER, HEAD_DIM)
    b_rows = b_in.astype(jnp.float32).reshape(blocks, TOK_DEV, GROUPS, STATE)
    c_rows = c_in.astype(jnp.float32).reshape(blocks, TOK_DEV, GROUPS, STATE)
    decays = log_decay.reshape(blocks, TOK_DEV, SCAN_LANE_NUMBER)
    step_rows = step_size.reshape(blocks, TOK_DEV, SCAN_LANE_NUMBER)

    def advance(state, block):
        block_x, block_b, block_c, block_decay, block_step = block
        within, cumulative, end_state, decay = local_terms(block_x, block_b, block_c, block_decay, block_step, per_group)
        output = within + carried(block_c, cumulative, state, per_group)
        return (decay[:, None, None] * state + end_state, output)
    start_state = jnp.zeros((SCAN_LANE_NUMBER, HEAD_DIM, STATE), jnp.float32)
    final_state, outputs = lax.scan(advance, start_state, (inputs, b_rows, c_rows, decays, step_rows))
    mixed = outputs.reshape(CONTEXT_SPAN, SCAN_LANE_NUMBER, HEAD_DIM) + d_skip[None, :, None] * x_in.astype(jnp.float32).reshape(CONTEXT_SPAN, SCAN_LANE_NUMBER, HEAD_DIM)
    gated = mixed.reshape(CONTEXT_SPAN, INNER) * jax.nn.silu(z_gate.astype(jnp.float32))
    grouped = gated.reshape(CONTEXT_SPAN, GROUPS, INNER // GROUPS)
    scaled = grouped * lax.rsqrt(lax.optimization_barrier(jnp.mean(grouped * grouped, axis=-1, keepdims=True)) + epsilon)
    normed_inner = (scaled.reshape(CONTEXT_SPAN, INNER) * norm_gain).astype(jnp.bfloat16)
    projected = jnp.dot(normed_inner, w_out, preferred_element_type=jnp.float32)
    hidden_out = residual.astype(jnp.float32) + projected
    normed = (hidden_out * lax.rsqrt(lax.optimization_barrier(jnp.mean(hidden_out * hidden_out, axis=-1, keepdims=True)) + epsilon) * final_gain).astype(jnp.bfloat16)

    def score(block):
        rows, wanted = block
        logits = lax.dot_general(rows, vocab, (((1,), (1,)), ((), ())), preferred_element_type=jnp.float32)
        picked = jnp.take_along_axis(logits, wanted[:, None], axis=1)[:, 0]
        return picked - jax.nn.logsumexp(logits, axis=1)
    logprob = lax.map(score, (normed.reshape(blocks, TOK_DEV, D), targets.reshape(blocks, TOK_DEV))).reshape(CONTEXT_SPAN)
    return (hidden_out, logprob)
```

```python
import jax
import jax.numpy as jnp
from jax import lax
from jax.experimental import pallas as pl
from jax.experimental.pallas import tpu as pltpu
from jax.sharding import Mesh, PartitionSpec as P

HEAD_DIM = 64
STATE = 256
CHAN = 1024
BLOCKS = 32
SLICE = STATE // BLOCKS
EXTRA = 128
HALF = jnp.float16
PART_SCALE = 512.0
TILE = 512

epsilon = 1e-05
highest = lax.Precision.HIGHEST
SEQ = ("z", "y")
HEAD = ("x", "core")


def pieces(value):
    value = value * 128.0
    first = lax.reduce_precision(value, 5, 10)
    second = lax.reduce_precision(value - first, 5, 10)
    third = value - first - second
    return [part.astype(HALF) for part in (first, second, third)]


def scan_kernel(recv_ref, out_ref):
    head_of = lax.broadcasted_iota(jnp.int32, (EXTRA, CHAN), 1) // HEAD_DIM
    spread = (head_of == lax.broadcasted_iota(jnp.int32, (EXTRA, CHAN), 0)).astype(jnp.float32)
    wide = jnp.dot(
        recv_ref[:, CHAN:],
        spread,
        precision=highest,
        preferred_element_type=jnp.float32,
    )
    state = jnp.zeros((SLICE, CHAN), jnp.float32)
    for block in range(BLOCKS):
        rows = slice(block * SLICE, (block + 1) * SLICE)
        out_ref[rows, :] = state
        last = wide[rows, :]
        decay = jnp.exp((last[0:1] + last[1:2] + last[2:3]) * (-1.0 / 128.0))
        state = decay * state + recv_ref[rows, :CHAN]


def scan_states(received):
    return pl.pallas_call(
        scan_kernel,
        out_shape=jax.ShapeDtypeStruct((STATE, CHAN), jnp.float32),
        name="scan_states",
    )(received.astype(jnp.float32)).astype(HALF)


def score_kernel(wanted_ref, token_ref, vocab_ref, out_ref, top_ref, total_ref, hit_ref):
    step = pl.program_id(0)
    count = token_ref.shape[0]

    @pl.when(step == 0)
    def _():
        top_ref[...] = jnp.full(top_ref.shape, -jnp.inf, jnp.float32)
        total_ref[...] = jnp.zeros(total_ref.shape, jnp.float32)
        hit_ref[...] = jnp.zeros(hit_ref.shape, jnp.float32)

    logits = lax.dot_general(
        vocab_ref[...],
        token_ref[...],
        (((1,), (1,)), ((), ())),
        preferred_element_type=jnp.float32,
    )
    ids = step * TILE + lax.broadcasted_iota(jnp.int32, logits.shape, 0)
    hit = jnp.where(ids == wanted_ref[...], logits, 0.0)
    hit_ref[...] += jnp.sum(hit.reshape(TILE // 8, 8, count), axis=0)
    folded = logits.reshape(TILE // 8, 8, count)
    old = top_ref[...]
    new = jnp.maximum(old, jnp.max(folded, axis=0))
    top_ref[...] = new
    total_ref[...] = total_ref[...] * jnp.exp(old - new) + jnp.sum(
        jnp.exp(folded - new[None]), axis=0
    )

    @pl.when(step == pl.num_programs(0) - 1)
    def _():
        lane_top = top_ref[...]
        top = jnp.max(lane_top, axis=0, keepdims=True)
        total = jnp.sum(total_ref[...] * jnp.exp(lane_top - top), axis=0, keepdims=True)
        picked = jnp.sum(hit_ref[...], axis=0, keepdims=True)
        row = lax.broadcasted_iota(jnp.int32, (8, count), 0)
        out_ref[...] = jnp.where(row == 0, top, jnp.where(row == 1, total, picked))


def score(wanted, token, vocab):
    count, width = token.shape
    entries = vocab.shape[0]
    return pl.pallas_call(
        score_kernel,
        grid=(entries // TILE,),
        in_specs=[
            pl.BlockSpec((1, count), lambda i: (0, 0)),
            pl.BlockSpec((count, width), lambda i: (0, 0)),
            pl.BlockSpec((TILE, width), lambda i: (i, 0)),
        ],
        out_specs=pl.BlockSpec((8, count), lambda i: (0, 0)),
        out_shape=jax.ShapeDtypeStruct((8, count), jnp.float32),
        scratch_shapes=[pltpu.VMEM((8, count), jnp.float32)] * 3,
        cost_estimate=pl.CostEstimate(
            flops=2 * count * width * entries,
            bytes_accessed=2 * (count + entries) * width,
            transcendentals=count * entries,
        ),
        name="score",
    )(wanted, token, vocab)


def exchange(value, axes):
    return lax.all_to_all(value, axes, split_axis=0, concat_axis=0, tiled=True)


def inner(
    x_in,
    z_gate,
    b_in,
    c_in,
    log_decay,
    step_size,
    d_skip,
    norm_gain,
    w_out,
    residual,
    final_gain,
    vocab,
    targets,
):
    length = x_in.shape[0]
    heads = log_decay.shape[1]
    vocab_all = lax.all_gather(vocab, HEAD, axis=0, tiled=True)

    inputs = x_in.astype(jnp.float32)
    cumulative = jnp.cumsum(log_decay, axis=0)
    last = cumulative[-1]
    end_weight = jnp.exp(last[None, :] - cumulative) * step_size
    weighted = inputs * jnp.repeat(end_weight, HEAD_DIM, axis=1)
    end_state = lax.dot_general(
        b_in.astype(jnp.float32), weighted, (((0,), (0,)), ((), ())), precision=highest
    ).astype(HALF)
    side = jnp.stack(pieces(last))
    side = jnp.pad(side, ((0, SLICE - 3), (0, EXTRA - heads)))
    side = jnp.broadcast_to(side[None], (BLOCKS, SLICE, EXTRA))
    payload = jnp.concatenate([end_state.reshape(BLOCKS, SLICE, CHAN), side], axis=-1)
    received = exchange(payload.reshape(STATE, CHAN + EXTRA), SEQ)
    incoming = exchange(scan_states(received), SEQ)

    by_head = cumulative.T
    gaps = by_head[:, None, :] - by_head[:, :, None]
    positions = jnp.arange(length)
    causal = positions[None, :] <= positions[:, None]
    segment_w = jnp.where(causal[None], jnp.exp(jnp.minimum(gaps, 0.0)), 0.0)
    scores = lax.dot_general(
        c_in, b_in, (((1,), (1,)), ((), ())), preferred_element_type=jnp.float32
    )
    weights = segment_w * scores[None] * step_size.T[:, None, :]
    within = jnp.einsum(
        "hts,shp->thp", weights, inputs.reshape(length, heads, HEAD_DIM), precision=highest
    ).reshape(length, CHAN)
    local = within + jnp.repeat(d_skip, HEAD_DIM)[None, :] * inputs

    carried = jnp.dot(c_in.astype(jnp.float32), incoming.astype(jnp.float32), precision=highest)
    mixed = local + jnp.repeat(jnp.exp(-cumulative), HEAD_DIM, axis=1) * carried
    gated = mixed * jax.nn.silu(z_gate.astype(jnp.float32))
    scaled = gated * lax.rsqrt(jnp.mean(gated * gated, axis=-1, keepdims=True) + epsilon)
    normed_inner = (scaled * norm_gain).astype(jnp.bfloat16)
    partial = jnp.dot(normed_inner, w_out, preferred_element_type=jnp.float32)
    parts = exchange((partial * PART_SCALE).astype(HALF), HEAD)
    rows = length // 8
    summed = jnp.sum(parts.reshape(8, rows, -1).astype(jnp.float32), axis=0) * (1.0 / PART_SCALE)
    hidden_out = residual.astype(jnp.float32) + summed
    normed = (
        hidden_out
        * lax.rsqrt(jnp.mean(hidden_out * hidden_out, axis=-1, keepdims=True) + epsilon)
        * final_gain
    ).astype(jnp.bfloat16)

    half = rows // 2
    near_a = exchange(jnp.concatenate([normed[:half]] * 4, axis=0), "y")
    token_a = lax.all_gather(near_a, "z", axis=0, tiled=True)
    far_b = exchange(jnp.concatenate([normed[half:]] * 8, axis=0), "z")
    token_b = exchange(jnp.concatenate([far_b] * 4, axis=0), "y")

    offset = lax.axis_index(SEQ) * vocab_all.shape[0]
    wanted = (targets - offset).reshape(8, 4, rows)
    wanted_a = wanted[:, :, :half].reshape(1, -1)
    wanted_b = wanted[:, :, half:].transpose(1, 0, 2).reshape(1, -1)
    found_a = score(wanted_a, token_a, vocab_all)
    found_b = score(wanted_b, token_b, vocab_all)
    found_a = found_a.reshape(8, 8, 4, half)
    found_b = found_b.reshape(8, 4, 8, half).transpose(0, 2, 1, 3)
    triple = jnp.concatenate([found_a, found_b], axis=-1).reshape(8, BLOCKS, rows)
    triple = jnp.pad(triple.transpose(1, 0, 2), ((0, 0), (0, 0), (0, 128 - rows)))
    triples = exchange(triple.reshape(BLOCKS * 8, 128), SEQ)
    triples = triples.reshape(BLOCKS, 8, 128)[:, :3, :rows]
    tops, totals, picks = triples[:, 0], triples[:, 1], triples[:, 2]
    best = jnp.max(tops, axis=0)
    whole = jnp.sum(totals * jnp.exp(tops - best[None]), axis=0)
    logprob = jnp.sum(picks, axis=0) - best - jnp.log(whole)
    return (hidden_out, logprob)


def solution(mesh):
    fine = Mesh(mesh.devices.reshape(8, 4, 4, 2), ("z", "y", "x", "core"))
    return jax.shard_map(
        inner,
        mesh=fine,
        in_specs=(
            P(SEQ, HEAD),
            P(SEQ, HEAD),
            P(SEQ, HEAD),
            P(SEQ, HEAD),
            P(SEQ, HEAD),
            P(SEQ, HEAD),
            P(HEAD),
            P(HEAD),
            P(HEAD, None),
            P(SEQ + HEAD, None),
            P(),
            P(SEQ + HEAD, None),
            P(None, HEAD),
        ),
        out_specs=(P(SEQ + HEAD, None), P(SEQ + HEAD)),
        check_vma=False,
    )
```

```python
import jax
import jax.numpy as jnp
from jax import lax
from jax.experimental import pallas as pl
from jax.experimental.pallas import tpu as pltpu
from jax.sharding import Mesh, PartitionSpec as P

HEAD_DIM = 64
STATE = 256
CHAN = 1024
BLOCKS = 32
SLICE = STATE // BLOCKS
EXTRA = 128
HALF = jnp.float16
PART_SCALE = 512.0
TILE = 512

epsilon = 1e-05
highest = lax.Precision.HIGHEST
SEQ = ("z", "y")
HEAD = ("x", "core")


def pieces(value):
    value = value * 128.0
    first = lax.reduce_precision(value, 5, 10)
    second = lax.reduce_precision(value - first, 5, 10)
    third = value - first - second
    return [part.astype(HALF) for part in (first, second, third)]


def scan_kernel(recv_ref, out_ref):
    head_of = lax.broadcasted_iota(jnp.int32, (EXTRA, CHAN), 1) // HEAD_DIM
    spread = (head_of == lax.broadcasted_iota(jnp.int32, (EXTRA, CHAN), 0)).astype(jnp.float32)
    last = jnp.sum(recv_ref[:, CHAN:].reshape(BLOCKS, SLICE, EXTRA), axis=1)
    decay = jnp.dot(
        jnp.exp(last * (-1.0 / 128.0)),
        spread,
        precision=highest,
        preferred_element_type=jnp.float32,
    )
    state = jnp.zeros((SLICE, CHAN), jnp.float32)
    for block in range(BLOCKS):
        rows = slice(block * SLICE, (block + 1) * SLICE)
        out_ref[rows, :] = state
        state = decay[block : block + 1] * state + recv_ref[rows, :CHAN]


def scan_states(received):
    return pl.pallas_call(
        scan_kernel,
        out_shape=jax.ShapeDtypeStruct((STATE, CHAN), jnp.float32),
        name="scan_states",
    )(received.astype(jnp.float32)).astype(HALF)


def score_kernel(*refs):
    wanted_ref, token_ref, vocab_ref = refs[:3]
    near_ref = refs[3] if len(refs) == 8 else None
    out_ref, top_ref, total_ref, hit_ref = refs[-4:]
    step = pl.program_id(0)
    count = token_ref.shape[0]

    @pl.when(step == 0)
    def _():
        top_ref[...] = jnp.full(top_ref.shape, -jnp.inf, jnp.float32)
        total_ref[...] = jnp.zeros(total_ref.shape, jnp.float32)
        hit_ref[...] = jnp.zeros(hit_ref.shape, jnp.float32)

    logits = lax.dot_general(
        vocab_ref[...],
        token_ref[...],
        (((1,), (1,)), ((), ())),
        preferred_element_type=jnp.float32,
    )
    ids = step * TILE + lax.broadcasted_iota(jnp.int32, logits.shape, 0)
    hit = jnp.where(ids == wanted_ref[...], logits, 0.0)
    hit_ref[...] += jnp.sum(hit.reshape(TILE // 8, 8, count), axis=0)
    folded = logits.reshape(TILE // 8, 8, count)
    old = top_ref[...]
    new = jnp.maximum(old, jnp.max(folded, axis=0))
    top_ref[...] = new
    total_ref[...] = total_ref[...] * jnp.exp(old - new) + jnp.sum(
        jnp.exp(folded - new[None]), axis=0
    )

    @pl.when(step == pl.num_programs(0) - 1)
    def _():
        lane_top = top_ref[...]
        top = jnp.max(lane_top, axis=0, keepdims=True)
        total = jnp.sum(total_ref[...] * jnp.exp(lane_top - top), axis=0, keepdims=True)
        picked = jnp.sum(hit_ref[...], axis=0, keepdims=True)
        row = lax.broadcasted_iota(jnp.int32, (128, count), 0) % 3
        packed = jnp.where(row == 0, top, jnp.where(row == 1, total, picked)).T
        if near_ref is None:
            out_ref[...] = packed
        else:
            lane = lax.broadcasted_iota(jnp.int32, (8, 128), 1)
            for z in range(8):
                for y in range(4):
                    there = pl.ds((z * 4 + y) * 8, 8)
                    here = (y * 8 + z) * 8
                    far = packed[here : here + 8]
                    out_ref[there, :] = jnp.where(lane < 3, near_ref[there, :], far)


def score(wanted, token, vocab, *near):
    count, width = token.shape
    entries = vocab.shape[0]
    return pl.pallas_call(
        score_kernel,
        grid=(entries // TILE,),
        in_specs=[
            pl.BlockSpec((1, count), lambda i: (0, 0)),
            pl.BlockSpec((count, width), lambda i: (0, 0)),
            pl.BlockSpec((TILE, width), lambda i: (i, 0)),
        ]
        + [pl.BlockSpec((count, 128), lambda i: (0, 0))] * len(near),
        out_specs=pl.BlockSpec((count, 128), lambda i: (0, 0)),
        out_shape=jax.ShapeDtypeStruct((count, 128), jnp.float32),
        scratch_shapes=[pltpu.VMEM((8, count), jnp.float32)] * 3,
        cost_estimate=pl.CostEstimate(
            flops=2 * count * width * entries,
            bytes_accessed=2 * (count + entries) * width,
            transcendentals=count * entries,
        ),
        compiler_params=pltpu.CompilerParams(vmem_limit_bytes=(48 if near else 52) * 2**20),
        name="score",
    )(wanted, token, vocab, *near)


def exchange(value, axes):
    return lax.all_to_all(value, axes, split_axis=0, concat_axis=0, tiled=True)


def inner(
    x_in,
    z_gate,
    b_in,
    c_in,
    log_decay,
    step_size,
    d_skip,
    norm_gain,
    w_out,
    residual,
    final_gain,
    vocab,
    targets,
):
    length = x_in.shape[0]
    heads = log_decay.shape[1]
    vocab_all = lax.all_gather(vocab, HEAD, axis=0, tiled=True)

    inputs = x_in.astype(jnp.float32)
    cumulative = jnp.cumsum(log_decay, axis=0)
    last = cumulative[-1]
    end_weight = jnp.exp(last[None, :] - cumulative) * step_size
    weighted = inputs * jnp.repeat(end_weight, HEAD_DIM, axis=1)
    end_state = lax.dot_general(
        b_in.astype(jnp.float32), weighted, (((0,), (0,)), ((), ())), precision=highest
    ).astype(HALF)
    side = jnp.stack(pieces(last))
    side = jnp.pad(side, ((0, SLICE - 3), (0, EXTRA - heads)))
    side = jnp.broadcast_to(side[None], (BLOCKS, SLICE, EXTRA))
    payload = jnp.concatenate([end_state.reshape(BLOCKS, SLICE, CHAN), side], axis=-1)
    received = exchange(payload.reshape(STATE, CHAN + EXTRA), SEQ)
    incoming = exchange(scan_states(received), SEQ)

    by_head = cumulative.T
    gaps = by_head[:, None, :] - by_head[:, :, None]
    positions = jnp.arange(length)
    causal = positions[None, :] <= positions[:, None]
    segment_w = jnp.where(causal[None], jnp.exp(jnp.minimum(gaps, 0.0)), 0.0)
    scores = lax.dot_general(
        c_in, b_in, (((1,), (1,)), ((), ())), preferred_element_type=jnp.float32
    )
    weights = segment_w * scores[None] * step_size.T[:, None, :]
    within = jnp.einsum(
        "hts,shp->thp", weights, inputs.reshape(length, heads, HEAD_DIM), precision=highest
    ).reshape(length, CHAN)
    local = within + jnp.repeat(d_skip, HEAD_DIM)[None, :] * inputs

    carried = jnp.dot(c_in.astype(jnp.float32), incoming.astype(jnp.float32), precision=highest)
    mixed = local + jnp.repeat(jnp.exp(-cumulative), HEAD_DIM, axis=1) * carried
    gated = mixed * jax.nn.silu(z_gate.astype(jnp.float32))
    scaled = gated * lax.rsqrt(jnp.mean(gated * gated, axis=-1, keepdims=True) + epsilon)
    normed_inner = (scaled * norm_gain).astype(jnp.bfloat16)
    partial = jnp.dot(normed_inner, w_out, preferred_element_type=jnp.float32)
    rows = length // 8
    swapped = (partial * PART_SCALE).astype(HALF).reshape(4, 2, rows, -1).transpose(1, 0, 2, 3)
    pair = exchange(swapped.reshape(length, -1), "core")
    pair = pair.reshape(2, length // 2, -1).astype(jnp.float32)
    pair = ((pair[0] + pair[1]) * 0.5).astype(HALF)
    parts = exchange(pair, "x")
    summed = jnp.sum(parts.reshape(4, rows, -1).astype(jnp.float32), axis=0) * (2.0 / PART_SCALE)
    hidden_out = residual.astype(jnp.float32) + summed
    normed = (
        hidden_out
        * lax.rsqrt(jnp.mean(hidden_out * hidden_out, axis=-1, keepdims=True) + epsilon)
        * final_gain
    ).astype(jnp.bfloat16)

    half = rows // 2
    near_a = exchange(jnp.concatenate([normed[:half]] * 4, axis=0), "y")
    token_a = lax.all_gather(near_a, "z", axis=0, tiled=True)
    far_b = exchange(jnp.concatenate([normed[half:]] * 8, axis=0), "z")
    token_b = exchange(jnp.concatenate([far_b] * 4, axis=0), "y")

    offset = lax.axis_index(SEQ) * vocab_all.shape[0]
    wanted = (targets - offset).reshape(8, 4, rows)
    wanted_a = wanted[:, :, :half].reshape(1, -1)
    wanted_b = wanted[:, :, half:].transpose(1, 0, 2).reshape(1, -1)
    found_a = score(wanted_a, token_a, vocab_all)
    triple = score(wanted_b, token_b, vocab_all, found_a)
    triples = exchange(triple, SEQ)
    triples = triples.reshape(BLOCKS, half, 128)[:, :, :6].reshape(BLOCKS, half, 2, 3)
    tops, totals, picks = triples[..., 0], triples[..., 1], triples[..., 2]
    best = jnp.max(tops, axis=0)
    whole = jnp.sum(totals * jnp.exp(tops - best[None]), axis=0)
    logprob = jnp.sum(picks, axis=0) - best - jnp.log(whole)
    return (hidden_out, logprob.T.reshape(rows))


def solution(mesh):
    fine = Mesh(mesh.devices.reshape(8, 4, 4, 2), ("z", "y", "x", "core"))
    return jax.shard_map(
        inner,
        mesh=fine,
        in_specs=(
            P(SEQ, HEAD),
            P(SEQ, HEAD),
            P(SEQ, HEAD),
            P(SEQ, HEAD),
            P(SEQ, HEAD),
            P(SEQ, HEAD),
            P(HEAD),
            P(HEAD),
            P(HEAD, None),
            P(SEQ + HEAD, None),
            P(),
            P(SEQ + HEAD, None),
            P(None, HEAD),
        ),
        out_specs=(P(SEQ + HEAD, None), P(SEQ + HEAD)),
        check_vma=False,
    )
```

```python
import jax
import jax.numpy as jnp
from jax import lax
from jax.experimental import pallas as pl
from jax.experimental.pallas import tpu as pltpu
from jax.sharding import Mesh, PartitionSpec as P

HEAD_DIM = 64
STATE = 256
CHAN = 1024
BLOCKS = 32
SLICE = STATE // BLOCKS
EXTRA = 128
HALF = jnp.float16
PART_SCALE = 512.0
TILE = 512
SPAN = 2048

epsilon = 1e-05
highest = lax.Precision.HIGHEST
SEQ = ("z", "y")
HEAD = ("x", "core")


def pieces(value):
    value = value * 128.0
    first = lax.reduce_precision(value, 5, 10)
    second = lax.reduce_precision(value - first, 5, 10)
    third = value - first - second
    return [part.astype(HALF) for part in (first, second, third)]


def scan_kernel(recv_ref, out_ref):
    head_of = lax.broadcasted_iota(jnp.int32, (EXTRA, CHAN), 1) // HEAD_DIM
    spread = (head_of == lax.broadcasted_iota(jnp.int32, (EXTRA, CHAN), 0)).astype(jnp.float32)
    last = jnp.sum(recv_ref[:, CHAN:].reshape(BLOCKS, SLICE, EXTRA), axis=1)
    decay = jnp.dot(
        jnp.exp(last * (-1.0 / 128.0)),
        spread,
        precision=highest,
        preferred_element_type=jnp.float32,
    )
    state = jnp.zeros((SLICE, CHAN), jnp.float32)
    for block in range(BLOCKS):
        rows = slice(block * SLICE, (block + 1) * SLICE)
        out_ref[rows, :] = state
        state = decay[block : block + 1] * state + recv_ref[rows, :CHAN]


def scan_states(received):
    return pl.pallas_call(
        scan_kernel,
        out_shape=jax.ShapeDtypeStruct((STATE, CHAN), jnp.float32),
        name="scan_states",
    )(received.astype(jnp.float32)).astype(HALF)


def score_kernel(*refs):
    wanted_ref, token_ref, vocab_ref = refs[:3]
    near_ref = refs[3] if len(refs) == 8 else None
    out_ref, top_ref, total_ref, hit_ref = refs[-4:]
    step = pl.program_id(0)
    count = token_ref.shape[0]

    @pl.when(step == 0)
    def _():
        top_ref[...] = jnp.full(top_ref.shape, -jnp.inf, jnp.float32)
        total_ref[...] = jnp.zeros(total_ref.shape, jnp.float32)
        hit_ref[...] = jnp.zeros(hit_ref.shape, jnp.float32)

    logits = lax.dot_general(
        vocab_ref[...],
        token_ref[...],
        (((1,), (1,)), ((), ())),
        preferred_element_type=jnp.float32,
    )
    ids = step * SPAN + lax.broadcasted_iota(jnp.int32, logits.shape, 0)
    hit = jnp.where(ids == wanted_ref[...], logits, 0.0)
    hit_ref[...] += jnp.sum(hit.reshape(TILE // 8, 8, count), axis=0)
    folded = logits.reshape(TILE // 8, 8, count)
    old = top_ref[...]
    new = jnp.maximum(old, jnp.max(folded, axis=0))
    top_ref[...] = new
    total_ref[...] = total_ref[...] * jnp.exp(old - new) + jnp.sum(
        jnp.exp(folded - new[None]), axis=0
    )

    @pl.when(step == pl.num_programs(0) - 1)
    def _():
        lane_top = top_ref[...]
        top = jnp.max(lane_top, axis=0, keepdims=True)
        total = jnp.sum(total_ref[...] * jnp.exp(lane_top - top), axis=0, keepdims=True)
        picked = jnp.sum(hit_ref[...], axis=0, keepdims=True)
        row = lax.broadcasted_iota(jnp.int32, (128, count), 0) % 3
        packed = jnp.where(row == 0, top, jnp.where(row == 1, total, picked)).T
        if near_ref is None:
            for z in range(8):
                for x in range(4):
                    here = (x * 8 + z) * 8
                    out_ref[pl.ds((z * 4 + x) * 8, 8), :] = packed[here : here + 8]
        else:
            lane = lax.broadcasted_iota(jnp.int32, packed.shape, 1)
            out_ref[...] = jnp.where(lane < 3, packed, near_ref[...])


def score(wanted, token, vocab, *near):
    count, width = token.shape
    entries = vocab.shape[0]
    return pl.pallas_call(
        score_kernel,
        grid=(entries // TILE,),
        in_specs=[
            pl.BlockSpec((1, count), lambda i: (0, 0)),
            pl.BlockSpec((count, width), lambda i: (0, 0)),
            pl.BlockSpec((TILE, width), lambda i: (i, 0)),
        ]
        + [pl.BlockSpec((count, 128), lambda i: (0, 0))] * len(near),
        out_specs=pl.BlockSpec((count, 128), lambda i: (0, 0)),
        out_shape=jax.ShapeDtypeStruct((count, 128), jnp.float32),
        scratch_shapes=[pltpu.VMEM((8, count), jnp.float32)] * 3,
        cost_estimate=pl.CostEstimate(
            flops=2 * count * width * entries,
            bytes_accessed=2 * (count + entries) * width,
            transcendentals=count * entries,
        ),
        compiler_params=pltpu.CompilerParams(vmem_limit_bytes=(52 if near else 48) * 2**20),
        name="score",
    )(wanted, token, vocab, *near)


def exchange(value, axes):
    return lax.all_to_all(value, axes, split_axis=0, concat_axis=0, tiled=True)


def inner(
    x_in,
    z_gate,
    b_in,
    c_in,
    log_decay,
    step_size,
    d_skip,
    norm_gain,
    w_out,
    residual,
    final_gain,
    vocab,
    targets,
):
    length = x_in.shape[0]
    heads = log_decay.shape[1]
    vocab_all = lax.all_gather(vocab, ("y", "core"), axis=0, tiled=True)

    inputs = x_in.astype(jnp.float32)
    cumulative = jnp.cumsum(log_decay, axis=0)
    last = cumulative[-1]
    end_weight = jnp.exp(last[None, :] - cumulative) * step_size
    weighted = inputs * jnp.repeat(end_weight, HEAD_DIM, axis=1)
    end_state = lax.dot_general(
        b_in.astype(jnp.float32), weighted, (((0,), (0,)), ((), ())), precision=highest
    ).astype(HALF)
    side = jnp.stack(pieces(last))
    side = jnp.pad(side, ((0, SLICE - 3), (0, EXTRA - heads)))
    side = jnp.broadcast_to(side[None], (BLOCKS, SLICE, EXTRA))
    payload = jnp.concatenate([end_state.reshape(BLOCKS, SLICE, CHAN), side], axis=-1)
    received = exchange(payload.reshape(STATE, CHAN + EXTRA), SEQ)
    incoming = exchange(scan_states(received), SEQ)

    by_head = cumulative.T
    gaps = by_head[:, None, :] - by_head[:, :, None]
    positions = jnp.arange(length)
    causal = positions[None, :] <= positions[:, None]
    segment_w = jnp.where(causal[None], jnp.exp(jnp.minimum(gaps, 0.0)), 0.0)
    scores = lax.dot_general(
        c_in, b_in, (((1,), (1,)), ((), ())), preferred_element_type=jnp.float32
    )
    weights = segment_w * scores[None] * step_size.T[:, None, :]
    within = jnp.einsum(
        "hts,shp->thp", weights, inputs.reshape(length, heads, HEAD_DIM), precision=highest
    ).reshape(length, CHAN)
    local = within + jnp.repeat(d_skip, HEAD_DIM)[None, :] * inputs

    carried = jnp.dot(c_in.astype(jnp.float32), incoming.astype(jnp.float32), precision=highest)
    mixed = local + jnp.repeat(jnp.exp(-cumulative), HEAD_DIM, axis=1) * carried
    gated = mixed * jax.nn.silu(z_gate.astype(jnp.float32))
    scaled = gated * lax.rsqrt(jnp.mean(gated * gated, axis=-1, keepdims=True) + epsilon)
    normed_inner = (scaled * norm_gain).astype(jnp.bfloat16)
    partial = jnp.dot(normed_inner, w_out, preferred_element_type=jnp.float32)
    rows = length // 8
    swapped = (partial * PART_SCALE).astype(HALF).reshape(4, 2, rows, -1).transpose(1, 0, 2, 3)
    pair = exchange(swapped.reshape(length, -1), "core")
    pair = pair.reshape(2, length // 2, -1).astype(jnp.float32)
    pair = ((pair[0] + pair[1]) * 0.5).astype(HALF).reshape(4, rows, -1)
    width = pair.shape[-1]
    ids = lax.dynamic_index_in_dim(targets.reshape(8, 4, rows), lax.axis_index("y"), 1, False)
    side = jnp.concatenate([ids // 256, ids % 256], axis=0).astype(HALF)
    side = jnp.broadcast_to(jnp.pad(side, ((0, 0), (0, EXTRA - rows)))[None], (4, rows, EXTRA))
    pair = jnp.concatenate([pair, side], axis=-1).reshape(length // 2, width + EXTRA)
    parts = exchange(pair, "x").reshape(4, rows, width + EXTRA).astype(jnp.float32)
    summed = jnp.sum(parts[:, :, :width], axis=0) * (2.0 / PART_SCALE)
    ids = parts[:, :, width : width + rows].astype(jnp.int32)
    ids = ids[:, :8] * 256 + ids[:, 8:]
    hidden_out = residual.astype(jnp.float32) + summed
    normed = (
        hidden_out
        * lax.rsqrt(jnp.mean(hidden_out * hidden_out, axis=-1, keepdims=True) + epsilon)
        * final_gain
    ).astype(jnp.bfloat16)

    half = rows // 2
    near_a = exchange(jnp.concatenate([normed[:half]] * 4, axis=0), "x")
    token_a = lax.all_gather(near_a, "z", axis=0, tiled=True)
    far_b = exchange(jnp.concatenate([normed[half:]] * 8, axis=0), "z")
    token_b = exchange(jnp.concatenate([far_b] * 4, axis=0), "x")

    ids = ids - (lax.axis_index("z") * (4 * SPAN) + lax.axis_index("x") * TILE)
    wanted_a = ids[:, :, :half].transpose(1, 0, 2).reshape(1, -1)
    wanted_b = ids[:, :, half:].reshape(1, -1)
    found_b = score(wanted_b, token_b, vocab_all)
    triple = score(wanted_a, token_a, vocab_all, found_b)
    triples = exchange(triple, ("z", "x"))
    triples = triples.reshape(BLOCKS, half, 128)[:, :, :6].reshape(BLOCKS, half, 2, 3)
    tops, totals, picks = triples[..., 0], triples[..., 1], triples[..., 2]
    best = jnp.max(tops, axis=0)
    whole = jnp.sum(totals * jnp.exp(tops - best[None]), axis=0)
    logprob = jnp.sum(picks, axis=0) - best - jnp.log(whole)
    return (hidden_out, logprob.T.reshape(rows))


def solution(mesh):
    fine = Mesh(mesh.devices.reshape(8, 4, 4, 2), ("z", "y", "x", "core"))
    return jax.shard_map(
        inner,
        mesh=fine,
        in_specs=(
            P(SEQ, HEAD),
            P(SEQ, HEAD),
            P(SEQ, HEAD),
            P(SEQ, HEAD),
            P(SEQ, HEAD),
            P(SEQ, HEAD),
            P(HEAD),
            P(HEAD),
            P(HEAD, None),
            P(SEQ + HEAD, None),
            P(),
            P(SEQ + HEAD, None),
            P(None, HEAD),
        ),
        out_specs=(P(SEQ + HEAD, None), P(SEQ + HEAD)),
        check_vma=False,
    )
```

```python
import functools

import jax
import jax.numpy as jnp
from jax import lax
from jax.experimental import pallas as pl
from jax.experimental.pallas import tpu as pltpu
from jax.sharding import Mesh, PartitionSpec as P

HEAD_DIM = 64
STATE = 256
CHAN = 1024
BLOCKS = 32
SLICE = STATE // BLOCKS
EXTRA = 128
HALF = jnp.float16
PART_SCALE = 512.0
TILE = 512
SPAN = 2048

epsilon = 1e-05
highest = lax.Precision.HIGHEST
SEQ = ("z", "y")
HEAD = ("x", "core")


def pieces(value):
    value = value * 128.0
    first = lax.reduce_precision(value, 5, 10)
    second = lax.reduce_precision(value - first, 5, 10)
    third = value - first - second
    return [part.astype(HALF) for part in (first, second, third)]


def scan_kernel(recv_ref, out_ref):
    head_of = lax.broadcasted_iota(jnp.int32, (EXTRA, CHAN), 1) // HEAD_DIM
    spread = (head_of == lax.broadcasted_iota(jnp.int32, (EXTRA, CHAN), 0)).astype(jnp.float32)
    last = jnp.sum(recv_ref[:, CHAN:].reshape(BLOCKS, SLICE, EXTRA), axis=1)
    decay = jnp.dot(
        jnp.exp(last * (-1.0 / 128.0)),
        spread,
        precision=highest,
        preferred_element_type=jnp.float32,
    )
    state = jnp.zeros((SLICE, CHAN), jnp.float32)
    for block in range(BLOCKS):
        rows = slice(block * SLICE, (block + 1) * SLICE)
        out_ref[rows, :] = state
        state = decay[block : block + 1] * state + recv_ref[rows, :CHAN]


def scan_states(received):
    return pl.pallas_call(
        scan_kernel,
        out_shape=jax.ShapeDtypeStruct((STATE, CHAN), jnp.float32),
        name="scan_states",
    )(received.astype(jnp.float32)).astype(HALF)


def score_kernel(*refs, count, parts):
    here_ref, wanted_ref, vocab_ref = refs[:3]
    token_refs = refs[3 : 3 + parts]
    if parts == 1:
        near_ref, out_ref, top_ref, total_ref, hit_ref = refs[4:]
        token_ref = token_refs[0]
    else:
        out_ref, top_ref, total_ref, hit_ref, token_ref = refs[3 + parts :]
    step = pl.program_id(0)

    @pl.when(step == 0)
    def _():
        top_ref[...] = jnp.full(top_ref.shape, -jnp.inf, jnp.float32)
        total_ref[...] = jnp.zeros(total_ref.shape, jnp.float32)
        hit_ref[...] = jnp.zeros(hit_ref.shape, jnp.float32)
        if parts > 1:
            at = 0
            for part_ref in token_refs:
                token_ref[at : at + part_ref.shape[0], :] = part_ref[...]
                at += part_ref.shape[0]

    logits = lax.dot_general(
        vocab_ref[...],
        token_ref[...],
        (((1,), (1,)), ((), ())),
        preferred_element_type=jnp.float32,
    )
    ids = step * SPAN + lax.broadcasted_iota(jnp.int32, logits.shape, 0)
    hit = jnp.where(ids == wanted_ref[...], logits, 0.0)
    hit_ref[...] += jnp.sum(hit.reshape(TILE // 8, 8, count), axis=0)
    folded = logits.reshape(TILE // 8, 8, count)
    old = top_ref[...]
    new = jnp.maximum(old, jnp.max(folded, axis=0))
    top_ref[...] = new
    total_ref[...] = total_ref[...] * jnp.exp(old - new) + jnp.sum(
        jnp.exp(folded - new[None]), axis=0
    )

    @pl.when(step == pl.num_programs(0) - 1)
    def _():
        lane_top = top_ref[...]
        top = jnp.max(lane_top, axis=0, keepdims=True)
        total = jnp.sum(total_ref[...] * jnp.exp(lane_top - top), axis=0, keepdims=True)
        picked = jnp.sum(hit_ref[...], axis=0, keepdims=True)
        row = lax.broadcasted_iota(jnp.int32, (128, count), 0) % 3
        packed = jnp.where(row == 0, top, jnp.where(row == 1, total, picked)).T
        if parts > 1:
            out_ref[...] = packed
        else:
            lane = lax.broadcasted_iota(jnp.int32, (8, 128), 1)
            for x in range(4):
                part = lax.rem(here_ref[0] + (4 - x), 4)
                for z in range(8):
                    at = (z * 4 + x) * 8
                    near = near_ref[pl.ds(pl.multiple_of(part * 64 + z * 8, 8), 8), :]
                    out_ref[pl.ds(at, 8), :] = jnp.where(lane < 3, packed[at : at + 8], near)


def score(here, wanted, tokens, vocab, *near):
    count = sum(token.shape[0] for token in tokens)
    entries, width = vocab.shape
    stats = [pltpu.VMEM((8, count), jnp.float32)] * 3
    return pl.pallas_call(
        functools.partial(score_kernel, count=count, parts=len(tokens)),
        grid=(entries // TILE,),
        in_specs=[
            pl.BlockSpec(memory_space=pltpu.SMEM),
            pl.BlockSpec((1, count), lambda i: (0, 0)),
            pl.BlockSpec((TILE, width), lambda i: (i, 0)),
        ]
        + [pl.BlockSpec(token.shape, lambda i: (0, 0)) for token in tokens]
        + [pl.BlockSpec((count, 128), lambda i: (0, 0))] * len(near),
        out_specs=pl.BlockSpec((count, 128), lambda i: (0, 0)),
        out_shape=jax.ShapeDtypeStruct((count, 128), jnp.float32),
        scratch_shapes=stats + [pltpu.VMEM((count, width), vocab.dtype)] * (len(tokens) > 1),
        cost_estimate=pl.CostEstimate(
            flops=2 * count * width * entries,
            bytes_accessed=2 * (count + entries) * width,
            transcendentals=count * entries,
        ),
        compiler_params=pltpu.CompilerParams(vmem_limit_bytes=(52 if near else 48) * 2**20),
        name="score",
    )(here.reshape(1), wanted, vocab, *tokens, *near)


def copies(value, count):
    return jnp.broadcast_to(value[None], (count,) + value.shape).reshape(-1, value.shape[1])


def exchange(value, axes):
    return lax.all_to_all(value, axes, split_axis=0, concat_axis=0, tiled=True)


def inner(
    x_in,
    z_gate,
    b_in,
    c_in,
    log_decay,
    step_size,
    d_skip,
    norm_gain,
    w_out,
    residual,
    final_gain,
    vocab,
    targets,
):
    length = x_in.shape[0]
    heads = log_decay.shape[1]
    vocab_all = lax.all_gather(vocab, ("y", "core"), axis=0, tiled=True)

    inputs = x_in.astype(jnp.float32)
    cumulative = jnp.cumsum(log_decay, axis=0)
    last = cumulative[-1]
    end_weight = jnp.exp(last[None, :] - cumulative) * step_size
    weighted = inputs * jnp.repeat(end_weight, HEAD_DIM, axis=1)
    end_state = lax.dot_general(
        b_in.astype(jnp.float32), weighted, (((0,), (0,)), ((), ())), precision=highest
    ).astype(HALF)
    side = jnp.stack(pieces(last))
    side = jnp.pad(side, ((0, SLICE - 3), (0, EXTRA - heads)))
    side = jnp.broadcast_to(side[None], (BLOCKS, SLICE, EXTRA))
    payload = jnp.concatenate([end_state.reshape(BLOCKS, SLICE, CHAN), side], axis=-1)
    received = exchange(payload.reshape(STATE, CHAN + EXTRA), SEQ)
    incoming = exchange(scan_states(received), SEQ)

    by_head = cumulative.T
    gaps = by_head[:, None, :] - by_head[:, :, None]
    positions = jnp.arange(length)
    causal = positions[None, :] <= positions[:, None]
    segment_w = jnp.where(causal[None], jnp.exp(jnp.minimum(gaps, 0.0)), 0.0)
    scores = lax.dot_general(
        c_in, b_in, (((1,), (1,)), ((), ())), preferred_element_type=jnp.float32
    )
    weights = segment_w * scores[None] * step_size.T[:, None, :]
    within = jnp.einsum(
        "hts,shp->thp", weights, inputs.reshape(length, heads, HEAD_DIM), precision=highest
    ).reshape(length, CHAN)
    local = within + jnp.repeat(d_skip, HEAD_DIM)[None, :] * inputs

    carried = jnp.dot(c_in.astype(jnp.float32), incoming.astype(jnp.float32), precision=highest)
    mixed = local + jnp.repeat(jnp.exp(-cumulative), HEAD_DIM, axis=1) * carried
    gated = mixed * jax.nn.silu(z_gate.astype(jnp.float32))
    scaled = gated * lax.rsqrt(jnp.mean(gated * gated, axis=-1, keepdims=True) + epsilon)
    normed_inner = (scaled * norm_gain).astype(jnp.bfloat16)
    partial = jnp.dot(normed_inner, w_out, preferred_element_type=jnp.float32)
    rows = length // 8
    swapped = (partial * PART_SCALE).astype(HALF).reshape(4, 2, rows, -1).transpose(1, 0, 2, 3)
    pair = exchange(swapped.reshape(length, -1), "core")
    pair = pair.reshape(2, length // 2, -1).astype(jnp.float32)
    pair = ((pair[0] + pair[1]) * 0.5).astype(HALF).reshape(4, rows, -1)
    width = pair.shape[-1]
    ids = lax.dynamic_index_in_dim(targets.reshape(8, 4, rows), lax.axis_index("y"), 1, False)
    side = jnp.concatenate([ids // 256, ids % 256], axis=0).astype(HALF)
    side = jnp.broadcast_to(jnp.pad(side, ((0, 0), (0, EXTRA - rows)))[None], (4, rows, EXTRA))
    pair = jnp.concatenate([pair, side], axis=-1).reshape(length // 2, width + EXTRA)
    parts = exchange(pair, "x").reshape(4, rows, width + EXTRA).astype(jnp.float32)
    summed = jnp.sum(parts[:, :, :width], axis=0) * (2.0 / PART_SCALE)
    ids = parts[:, :, width : width + rows].astype(jnp.int32)
    ids = ids[:, :8] * 256 + ids[:, 8:]
    hidden_out = residual.astype(jnp.float32) + summed
    normed = (
        hidden_out
        * lax.rsqrt(jnp.mean(hidden_out * hidden_out, axis=-1, keepdims=True) + epsilon)
        * final_gain
    ).astype(jnp.bfloat16)

    half = rows // 2
    near_a = exchange(copies(normed[:half], 4), "x")
    token_a = lax.all_gather(near_a, "z", axis=0, tiled=True)
    far_b = exchange(copies(normed[half:], 8), "z")
    up = [(i, (i + 1) % 4) for i in range(4)]
    down = [(i, (i - 1) % 4) for i in range(4)]
    quarter = far_b.shape[0] // 2
    one_up = lax.ppermute(far_b, "x", up)
    one_down = lax.ppermute(far_b, "x", down)
    two_up = lax.ppermute(one_up[:quarter], "x", up)
    two_down = lax.ppermute(one_down[quarter:], "x", down)
    token_b = (far_b, one_up, two_up, two_down, one_down)

    ids = ids - (lax.axis_index("z") * (4 * SPAN) + lax.axis_index("x") * TILE)
    wanted_a = ids[:, :, :half].transpose(1, 0, 2).reshape(1, -1)
    here = lax.axis_index("x")
    wanted_b = jnp.take(ids, (here - jnp.arange(4)) % 4, axis=0)[:, :, half:].reshape(1, -1)
    found_b = score(here, wanted_b, token_b, vocab_all)
    triple = score(here, wanted_a, (token_a,), vocab_all, found_b)
    triples = exchange(triple, ("z", "x"))
    triples = triples.reshape(BLOCKS, half, 128)[:, :, :6].reshape(BLOCKS, half, 2, 3)
    tops, totals, picks = triples[..., 0], triples[..., 1], triples[..., 2]
    best = jnp.max(tops, axis=0)
    whole = jnp.sum(totals * jnp.exp(tops - best[None]), axis=0)
    logprob = jnp.sum(picks, axis=0) - best - jnp.log(whole)
    return (hidden_out, logprob.T.reshape(rows))


def solution(mesh):
    fine = Mesh(mesh.devices.reshape(8, 4, 4, 2), ("z", "y", "x", "core"))
    return jax.shard_map(
        inner,
        mesh=fine,
        in_specs=(
            P(SEQ, HEAD),
            P(SEQ, HEAD),
            P(SEQ, HEAD),
            P(SEQ, HEAD),
            P(SEQ, HEAD),
            P(SEQ, HEAD),
            P(HEAD),
            P(HEAD),
            P(HEAD, None),
            P(SEQ + HEAD, None),
            P(),
            P(SEQ + HEAD, None),
            P(None, HEAD),
        ),
        out_specs=(P(SEQ + HEAD, None), P(SEQ + HEAD)),
        check_vma=False,
    )
```

```python
import functools

import jax
import jax.numpy as jnp
from jax import lax
from jax.experimental import pallas as pl
from jax.experimental.pallas import tpu as pltpu
from jax.sharding import Mesh, PartitionSpec as P

HEAD_DIM = 64
STATE = 256
CHAN = 1024
BLOCKS = 32
SLICE = STATE // BLOCKS
EXTRA = 128
HALF = jnp.float16
PART_SCALE = 512.0
TILE = 512
SPAN = 2048

epsilon = 1e-05
highest = lax.Precision.HIGHEST
SEQ = ("z", "y")
HEAD = ("x", "core")


def pieces(value):
    value = value * 128.0
    first = lax.reduce_precision(value, 5, 10)
    second = lax.reduce_precision(value - first, 5, 10)
    third = value - first - second
    return [part.astype(HALF) for part in (first, second, third)]


def scan_kernel(recv_ref, out_ref):
    head_of = lax.broadcasted_iota(jnp.int32, (EXTRA, CHAN), 1) // HEAD_DIM
    spread = (head_of == lax.broadcasted_iota(jnp.int32, (EXTRA, CHAN), 0)).astype(jnp.float32)
    last = jnp.sum(recv_ref[:, CHAN:].reshape(BLOCKS, SLICE, EXTRA), axis=1)
    decay = jnp.dot(
        jnp.exp(last * (-1.0 / 128.0)),
        spread,
        precision=highest,
        preferred_element_type=jnp.float32,
    )
    state = jnp.zeros((SLICE, CHAN), jnp.float32)
    for block in range(BLOCKS):
        rows = slice(block * SLICE, (block + 1) * SLICE)
        out_ref[rows, :] = state
        state = decay[block : block + 1] * state + recv_ref[rows, :CHAN]


def scan_states(received):
    return pl.pallas_call(
        scan_kernel,
        out_shape=jax.ShapeDtypeStruct((STATE, CHAN), jnp.float32),
        name="scan_states",
    )(received.astype(jnp.float32)).astype(HALF)


def score_kernel(*refs, count, parts):
    here_ref, wanted_ref, vocab_ref = refs[:3]
    token_refs = refs[3 : 3 + parts]
    if parts == 1:
        near_ref, out_ref, top_ref, total_ref, hit_ref = refs[4:]
        token_ref = token_refs[0]
    else:
        out_ref, top_ref, total_ref, hit_ref, token_ref = refs[3 + parts :]
    step = pl.program_id(0)

    @pl.when(step == 0)
    def _():
        top_ref[...] = jnp.full(top_ref.shape, -jnp.inf, jnp.float32)
        total_ref[...] = jnp.zeros(total_ref.shape, jnp.float32)
        hit_ref[...] = jnp.zeros(hit_ref.shape, jnp.float32)
        if parts > 1:
            at = 0
            for part_ref in token_refs:
                token_ref[at : at + part_ref.shape[0], :] = part_ref[...]
                at += part_ref.shape[0]

    logits = lax.dot_general(
        vocab_ref[...],
        token_ref[...],
        (((1,), (1,)), ((), ())),
        preferred_element_type=jnp.float32,
    )
    ids = step * SPAN + lax.broadcasted_iota(jnp.int32, logits.shape, 0)
    hit = jnp.where(ids == wanted_ref[...], logits, 0.0)
    hit_ref[...] += jnp.sum(hit.reshape(TILE // 8, 8, count), axis=0)
    folded = logits.reshape(TILE // 8, 8, count)
    old = top_ref[...]
    new = jnp.maximum(old, jnp.max(folded, axis=0))
    top_ref[...] = new
    total_ref[...] = total_ref[...] * jnp.exp(old - new) + jnp.sum(
        jnp.exp(folded - new[None]), axis=0
    )

    @pl.when(step == pl.num_programs(0) - 1)
    def _():
        lane_top = top_ref[...]
        top = jnp.max(lane_top, axis=0, keepdims=True)
        total = jnp.sum(total_ref[...] * jnp.exp(lane_top - top), axis=0, keepdims=True)
        picked = jnp.sum(hit_ref[...], axis=0, keepdims=True)
        row = lax.broadcasted_iota(jnp.int32, (128, count), 0) % 3
        packed = jnp.where(row == 0, top, jnp.where(row == 1, total, picked)).T
        if parts > 1:
            out_ref[...] = packed
        else:
            lane = lax.broadcasted_iota(jnp.int32, (8, 128), 1)
            for x in range(4):
                part = lax.rem(here_ref[0] + (4 - x), 4)
                for z in range(8):
                    at = (z * 4 + x) * 8
                    near = near_ref[pl.ds(pl.multiple_of(part * 64 + z * 8, 8), 8), :]
                    out_ref[pl.ds(at, 8), :] = jnp.where(lane < 3, packed[at : at + 8], near)


def score(here, wanted, tokens, vocab, *near):
    count = sum(token.shape[0] for token in tokens)
    entries, width = vocab.shape
    stats = [pltpu.VMEM((8, count), jnp.float32)] * 3
    return pl.pallas_call(
        functools.partial(score_kernel, count=count, parts=len(tokens)),
        grid=(entries // TILE,),
        in_specs=[
            pl.BlockSpec(memory_space=pltpu.SMEM),
            pl.BlockSpec((1, count), lambda i: (0, 0)),
            pl.BlockSpec((TILE, width), lambda i: (i, 0)),
        ]
        + [pl.BlockSpec(token.shape, lambda i: (0, 0)) for token in tokens]
        + [pl.BlockSpec((count, 128), lambda i: (0, 0))] * len(near),
        out_specs=pl.BlockSpec((count, 128), lambda i: (0, 0)),
        out_shape=jax.ShapeDtypeStruct((count, 128), jnp.float32),
        scratch_shapes=stats + [pltpu.VMEM((count, width), vocab.dtype)] * (len(tokens) > 1),
        cost_estimate=pl.CostEstimate(
            flops=2 * count * width * entries,
            bytes_accessed=2 * (count + entries) * width,
            transcendentals=count * entries,
        ),
        compiler_params=pltpu.CompilerParams(vmem_limit_bytes=(52 if near else 48) * 2**20),
        name="score",
    )(here.reshape(1), wanted, vocab, *tokens, *near)


def copies(value, count):
    return jnp.broadcast_to(value[None], (count,) + value.shape).reshape(-1, value.shape[1])


def exchange(value, axes):
    return lax.all_to_all(value, axes, split_axis=0, concat_axis=0, tiled=True)


def inner(
    x_in,
    z_gate,
    b_in,
    c_in,
    log_decay,
    step_size,
    d_skip,
    norm_gain,
    w_out,
    residual,
    final_gain,
    vocab,
    targets,
):
    length = x_in.shape[0]
    heads = log_decay.shape[1]
    vocab_all = lax.all_gather(vocab, ("y", "core"), axis=0, tiled=True)

    inputs = x_in.astype(jnp.float32)
    cumulative = jnp.cumsum(log_decay, axis=0)
    last = cumulative[-1]
    end_weight = jnp.exp(last[None, :] - cumulative) * step_size
    weighted = inputs * jnp.repeat(end_weight, HEAD_DIM, axis=1)
    end_state = lax.dot_general(
        b_in.astype(jnp.float32), weighted, (((0,), (0,)), ((), ())), precision=highest
    ).astype(HALF)
    side = jnp.stack(pieces(last))
    side = jnp.pad(side, ((0, SLICE - 3), (0, EXTRA - heads)))
    side = jnp.broadcast_to(side[None], (BLOCKS, SLICE, EXTRA))
    payload = jnp.concatenate([end_state.reshape(BLOCKS, SLICE, CHAN), side], axis=-1)
    received = exchange(payload.reshape(STATE, CHAN + EXTRA), SEQ)
    incoming = exchange(scan_states(received), SEQ)

    by_head = cumulative.T
    gaps = by_head[:, None, :] - by_head[:, :, None]
    positions = jnp.arange(length)
    causal = positions[None, :] <= positions[:, None]
    segment_w = jnp.where(causal[None], jnp.exp(jnp.minimum(gaps, 0.0)), 0.0)
    scores = lax.dot_general(
        c_in, b_in, (((1,), (1,)), ((), ())), preferred_element_type=jnp.float32
    )
    weights = segment_w * scores[None] * step_size.T[:, None, :]
    within = jnp.einsum(
        "hts,shp->thp", weights, inputs.reshape(length, heads, HEAD_DIM), precision=highest
    ).reshape(length, CHAN)
    local = within + jnp.repeat(d_skip, HEAD_DIM)[None, :] * inputs

    carried = jnp.dot(c_in.astype(jnp.float32), incoming.astype(jnp.float32), precision=highest)
    mixed = local + jnp.repeat(jnp.exp(-cumulative), HEAD_DIM, axis=1) * carried
    gated = mixed * jax.nn.silu(z_gate.astype(jnp.float32))
    scaled = gated * lax.rsqrt(jnp.mean(gated * gated, axis=-1, keepdims=True) + epsilon)
    normed_inner = (scaled * norm_gain).astype(jnp.bfloat16)
    partial = jnp.dot(normed_inner, w_out, preferred_element_type=jnp.float32)
    rows = length // 8
    swapped = (partial * PART_SCALE).astype(HALF).reshape(4, 2, rows, -1).transpose(1, 0, 2, 3)
    pair = exchange(swapped.reshape(length, -1), "core")
    pair = pair.reshape(2, length // 2, -1).astype(jnp.float32)
    pair = ((pair[0] + pair[1]) * 0.5).astype(HALF).reshape(4, rows, -1)
    width = pair.shape[-1]
    ids = lax.dynamic_index_in_dim(targets.reshape(8, 4, rows), lax.axis_index("y"), 1, False)
    side = jnp.concatenate([ids // 256, ids % 256], axis=0).astype(HALF)
    side = jnp.broadcast_to(jnp.pad(side, ((0, 0), (0, EXTRA - rows)))[None], (4, rows, EXTRA))
    pair = jnp.concatenate([pair, side], axis=-1).reshape(length // 2, width + EXTRA)
    parts = exchange(pair, "x").reshape(4, rows, width + EXTRA).astype(jnp.float32)
    summed = jnp.sum(parts[:, :, :width], axis=0) * (2.0 / PART_SCALE)
    ids = parts[:, :, width : width + rows].astype(jnp.int32)
    ids = ids[:, :8] * 256 + ids[:, 8:]
    hidden_out = residual.astype(jnp.float32) + summed
    normed = (
        hidden_out
        * lax.rsqrt(jnp.mean(hidden_out * hidden_out, axis=-1, keepdims=True) + epsilon)
        * final_gain
    ).astype(jnp.bfloat16)

    half = rows // 2
    here = lax.axis_index("x")
    up = [(i, (i + 1) % 4) for i in range(4)]
    across = [(i, (i + 2) % 4) for i in range(4)]
    down = [(i, (i - 1) % 4) for i in range(4)]
    first = normed[:half]
    near_a = jnp.stack(
        [first] + [lax.ppermute(first, "x", way) for way in (up, across, down)]
    )
    near_a = jnp.take(near_a, (here - jnp.arange(4)) % 4, axis=0).reshape(4 * half, -1)
    token_a = lax.all_gather(near_a, "z", axis=0, tiled=True)
    far_b = exchange(copies(normed[half:], 8), "z")
    quarter = far_b.shape[0] // 2
    one_up = lax.ppermute(far_b, "x", up)
    one_down = lax.ppermute(far_b, "x", down)
    two_up = lax.ppermute(one_up[:quarter], "x", up)
    two_down = lax.ppermute(one_down[quarter:], "x", down)
    token_b = (far_b, one_up, two_up, two_down, one_down)

    ids = ids - (lax.axis_index("z") * (4 * SPAN) + lax.axis_index("x") * TILE)
    wanted_a = ids[:, :, :half].transpose(1, 0, 2).reshape(1, -1)
    wanted_b = jnp.take(ids, (here - jnp.arange(4)) % 4, axis=0)[:, :, half:].reshape(1, -1)
    found_b = score(here, wanted_b, token_b, vocab_all)
    triple = score(here, wanted_a, (token_a,), vocab_all, found_b)
    triples = exchange(triple, ("z", "x"))
    triples = triples.reshape(BLOCKS, half, 128)[:, :, :6].reshape(BLOCKS, half, 2, 3)
    tops, totals, picks = triples[..., 0], triples[..., 1], triples[..., 2]
    best = jnp.max(tops, axis=0)
    whole = jnp.sum(totals * jnp.exp(tops - best[None]), axis=0)
    logprob = jnp.sum(picks, axis=0) - best - jnp.log(whole)
    return (hidden_out, logprob.T.reshape(rows))


def solution(mesh):
    fine = Mesh(mesh.devices.reshape(8, 4, 4, 2), ("z", "y", "x", "core"))
    return jax.shard_map(
        inner,
        mesh=fine,
        in_specs=(
            P(SEQ, HEAD),
            P(SEQ, HEAD),
            P(SEQ, HEAD),
            P(SEQ, HEAD),
            P(SEQ, HEAD),
            P(SEQ, HEAD),
            P(HEAD),
            P(HEAD),
            P(HEAD, None),
            P(SEQ + HEAD, None),
            P(),
            P(SEQ + HEAD, None),
            P(None, HEAD),
        ),
        out_specs=(P(SEQ + HEAD, None), P(SEQ + HEAD)),
        check_vma=False,
    )
```
